128 devices in a mesh: dp: 8 (over x, core), expert: 16 (over z, y).
Axes of the slice: x: 4, y: 4, z: 4, core: 2. Of those that a mesh axis runs over, the one named last changes fastest.
Arguments:
- tokens: bfloat16 [16384, 2048], P(('dp', 'expert')), may hold values from -6 to 6
- routes: int32 [16384, 2], P(('dp', 'expert')), may hold values from 0 to 31, all different within a row; in each aligned block of 128 rows (0 to 127, 128 to 255, ...) at most 10 rows name the same one
- gate_fixed: int32 [16384, 2], P(('dp', 'expert')), may hold values from 8192 to 57344
- up_weight: bfloat16 [32, 2048, 7168], P('expert', None, 'dp'), may hold values from -0.125 to 0.125
- up_mask: int32 [32, 16, 56], P('expert', None, 'dp'), may hold values 0 or 1
- down_weight: bfloat16 [32, 7168, 2048], P('expert', 'dp'), may hold values from -0.0625 to 0.0625
- down_mask: int32 [32, 56, 16], P('expert', 'dp'), may hold values 0 or 1
- threshold: int32 [32, 7168], P('expert', 'dp'), may hold values from 1 to 8
- cotangent: bfloat16 [16384, 2048], P('dp', 'expert'), may hold values from -6 to 6
Outputs:
- mixed: bfloat16 [16384, 2048], P('dp', 'expert')
- gate_grad: float32 [16384, 2], P(('dp', 'expert'))
- potential_grad: bfloat16 [1280, 32, 7168], P(None, 'expert', 'dp')
The draws below stay inside these ranges and needn't reach their ends.
Inputs may be any that keep to these rules, and one draw needn't show every extreme that they name: In each aligned block of 128 rows, no expert is named by more than 10 rows, a bound that some block reaches; the two routes of a token differ.
All inputs are finite; a program needn't handle non-finite values. No bound on the sum of `up_mask` or of `down_mask` on one device may be relied on, other than what follows from the above.
Results may differ from the reference program's by a relative error of at most 0.02.
Values may be sent and summed in bfloat16 or wider, within the bound.
No kernel may reach another device: no remote copies, remote signals or barrier semaphores. Data moves between devices by JAX's collectives and lax.ppermute only.
A program may use at most 192 MiB of HBM per device.

```python
import math
import jax
import jax.numpy as jnp
import numpy as np
from jax import lax

D = 2048
FFW = 7168
BLOCK = 128
TOK_DEV = 128
EXPERTS = 32
CAP = 10
TOKENS = 16384
N_DP = 8
N_EXPERT = 16


def with_ends(values, own_key, low, top_value):
    shape = values.shape
    index_at = [jax.random.randint(jax.random.fold_in(own_key, axis), (), 0, shape[axis]) for axis in range(len(shape))]
    values = values.at[tuple(index_at)].set(low)
    longest = shape.index(max(shape))
    index_at[longest] = (index_at[longest] + 1) % shape[longest]
    return values.at[tuple(index_at)].set(top_value)


def level_of(key, extent, shards, least, largest):
    def one(dim, parts):
        heights = jax.random.uniform(jax.random.fold_in(jax.random.fold_in(key, 6), dim), (parts,), jnp.float32, least / len(shards), largest / len(shards))
        return jnp.repeat(jnp.exp(heights), extent[dim] // parts).reshape((-1,) + (1,) * (len(extent) - dim - 1))

    level = one(*shards[0])
    for cut in shards[1:]:
        level = level * one(*cut)
    return level


def routed_block(own_key, own, number, rows, amount, top, limit, lean):
    ranking = jax.random.permutation(own_key, amount)
    heavy_load, usual = shares(amount, rows * top, limit, lean, True), shares(amount, rows * top, limit, lean, False)
    places = jnp.arange(amount)

    def named(sizes, turn):
        used = int((sizes > 0).sum())
        fixed = max(1, used // 4)
        shifted = fixed + (places - fixed + turn * (used - fixed)) % max(1, amount - fixed)
        return jnp.zeros((amount,), jnp.int32).at[ranking[jnp.where(places < fixed, places, shifted)]].set(jnp.asarray(sizes, jnp.int32))

    sizes = jnp.where(number % 4 == 0, named(heavy_load, number // 4), named(usual, number - number // 4 - 1))
    mixed = jax.random.permutation(jax.random.fold_in(own, 3), amount)
    source_of, taker = mixed[0:amount // 2 * 2:2], mixed[1:amount // 2 * 2:2]
    margin = jnp.minimum(sizes[source_of] - 1, limit - sizes[taker]) // 2
    margin = jnp.where((source_of == ranking[0]) | (taker == ranking[0]) | (sizes[taker] == 0), 0, jnp.maximum(margin, 0))
    shifted = jax.random.randint(jax.random.fold_in(own, 4), (amount // 2,), 0, 1 << 20) % (margin + 1)
    sizes = sizes.at[source_of].add(-shifted).at[taker].add(shifted)
    members = jnp.searchsorted(jnp.cumsum(sizes), jnp.arange(rows * top), side="right").astype(jnp.int32)
    grid = members.reshape(top, rows).T
    grid = grid[jax.random.permutation(jax.random.fold_in(own, 1), rows)]
    turn = jax.random.randint(jax.random.fold_in(own, 2), (rows, 1), 0, top)
    return jnp.take_along_axis(grid, (jnp.arange(top)[None, :] + turn) % top, axis=1)


def shares(count, total, bound, lean, full):
    weights = [(1 << 20) // math.isqrt(rank ** lean) + 1 for rank in range(1, count + 1)]
    largest = bound if full else min(bound, max(-(-total // count), total * weights[0] // sum(weights)))
    least = 1 if total - largest >= count - 1 else 0
    counts, surplus = [largest] + [least] * (count - 1), total - largest - least * (count - 1)
    while surplus > 0:
        candidates = [i for i in range(1, count) if counts[i] < largest] or [i for i in range(1, count) if counts[i] < bound]
        whole, budget = sum([weights[i] for i in candidates]), surplus
        for i in candidates:
            extra = min(bound - counts[i], max(1, budget * weights[i] // whole), surplus)
            counts[i] = counts[i] + extra
            surplus = surplus - extra
    return np.array(counts)


def scatter_about(own_key, shape, scale, reach, pieces=(), held_as=jnp.bfloat16):
    level = level_of(own_key, shape, pieces, -0.22, 0.18) if pieces else 1.0
    result = jax.random.normal(own_key, shape, jnp.float32) * scale * level
    return jnp.minimum(jnp.maximum(result, -reach), reach).astype(held_as)


def setup_inputs(seed: int = 0) -> dict:
    keys = jax.random.split(jax.random.key(seed), 10)
    tokens = scatter_about(keys[0], (TOKENS, D), 1.0, 6.0, ((0, 128),))
    routes_keys = jax.random.split(jax.random.fold_in(keys[1], 1), TOKENS // TOK_DEV)
    routes_turns = jax.random.permutation(jax.random.fold_in(keys[1], 3), TOKENS // TOK_DEV)
    routes = jax.vmap(lambda own, number: routed_block(jax.random.fold_in(keys[1], 2), own, number, TOK_DEV, EXPERTS, 2, CAP, 2))(routes_keys, routes_turns).reshape((TOKENS, 2))
    gate_fixed = with_ends(jax.random.randint(keys[2], (TOKENS, 2), 8192, 57345), jax.random.fold_in(keys[2], 1), 8192, 57344).astype(jnp.int32)
    up_weight = scatter_about(keys[3], (EXPERTS, D, FFW), D ** -0.5, 0.125, ((0, 16), (2, 8)))
    up_mask = with_ends((jax.random.randint(keys[4], (EXPERTS, D // BLOCK, FFW // BLOCK), 0, 4) < 3).astype(jnp.int32), jax.random.fold_in(keys[4], 1), 0, 1)
    down_weight = scatter_about(keys[5], (EXPERTS, FFW, D), FFW ** -0.5, 0.0625, ((0, 16), (1, 8)))
    down_mask = with_ends((jax.random.randint(keys[6], (EXPERTS, FFW // BLOCK, D // BLOCK), 0, 4) < 3).astype(jnp.int32), jax.random.fold_in(keys[6], 1), 0, 1)
    threshold = with_ends(jax.random.randint(keys[7], (EXPERTS, FFW), 1, 9), jax.random.fold_in(keys[7], 1), 1, 8).astype(jnp.int32)
    cotangent = scatter_about(keys[8], (TOKENS, D), 1.0, 6.0, ((0, 8), (1, 16)))
    return dict(tokens=tokens, routes=routes, gate_fixed=gate_fixed, up_weight=up_weight, up_mask=up_mask, down_weight=down_weight, down_mask=down_mask, threshold=threshold, cotangent=cotangent)


def widen(mask):
    return jnp.repeat(jnp.repeat(mask, BLOCK, axis=0), BLOCK, axis=1)

def reference(tokens, routes, gate_fixed, up_weight, up_mask, down_weight, down_mask, threshold, cotangent):
    blocks = N_DP * N_EXPERT
    flat_routes = routes.reshape(blocks, TOK_DEV * 2)
    onehot = (flat_routes[:, :, None] == jnp.arange(EXPERTS, dtype=jnp.int32)[None, None, :]).astype(jnp.int32)
    earlier = jnp.cumsum(onehot, axis=1) - onehot
    slots = lax.optimization_barrier(jnp.sum(onehot * earlier, axis=2))
    source = jnp.broadcast_to(jnp.arange(blocks, dtype=jnp.int32)[:, None], flat_routes.shape)
    place = (flat_routes * (blocks * CAP) + source * CAP + slots).reshape(-1).astype(jnp.int32)
    token_of = (jnp.arange(TOKENS * 2, dtype=jnp.int32) // 2).astype(jnp.int32)
    rows = jnp.zeros((EXPERTS * blocks * CAP, D), tokens.dtype).at[place].set(tokens[token_of])
    rows = rows.reshape(EXPERTS, blocks * CAP, D)
    scale = 4.0 / threshold.astype(jnp.float32)
    width_dp = FFW // N_DP

    def forward(args):
        x_rows, w_up, m_up, w_down, m_down, scl = args
        w_up = w_up * widen(m_up).astype(w_up.dtype)
        w_down = w_down * widen(m_down).astype(w_down.dtype)
        potential = jnp.dot(x_rows, w_up, preferred_element_type=jnp.float32)
        sig = jax.nn.sigmoid(potential)
        hidden = (potential * sig * scl[None, :]).astype(jnp.bfloat16)
        slope = (sig * (1.0 + potential * (1.0 - sig)) * scl[None, :]).astype(jnp.bfloat16)
        groups = hidden.reshape(-1, N_DP, width_dp).astype(jnp.float32)
        w_groups = w_down.reshape(N_DP, width_dp, D).astype(jnp.float32)
        part = jnp.einsum('rnf,nfd->nrd', groups, w_groups).astype(jnp.bfloat16)
        out = lax.optimization_barrier(jnp.sum(part.astype(jnp.float32), axis=0)).astype(jnp.bfloat16)
        return (out, slope)
    expert_out, slopes = lax.map(forward, (rows, up_weight, up_mask, down_weight, down_mask, scale))
    picked = expert_out.reshape(-1, D)[place].reshape(TOKENS, 2, D)
    gates = gate_fixed.astype(jnp.float32) / 65536.0
    mixed = lax.optimization_barrier(jnp.sum(gates[:, :, None] * picked.astype(jnp.float32), axis=1)).astype(jnp.bfloat16)
    cot = cotangent.astype(jnp.float32)
    gate_grad = lax.optimization_barrier(jnp.sum(cot[:, None, :] * picked.astype(jnp.float32), axis=2)) / math.sqrt(D)
    scaled = (gates[:, :, None] * cot[:, None, :]).astype(jnp.bfloat16).reshape(TOKENS * 2, D)
    grad_rows = jnp.zeros((EXPERTS * blocks * CAP, D), jnp.bfloat16).at[place].set(scaled)
    grad_rows = grad_rows.reshape(EXPERTS, blocks * CAP, D)

    def backward(args):
        g_rows, w_down, m_down, slope = args
        w_down = w_down * widen(m_down).astype(w_down.dtype)
        back = jnp.dot(g_rows, w_down.T, preferred_element_type=jnp.float32)
        return (back * slope.astype(jnp.float32)).astype(jnp.bfloat16)
    grads = lax.map(backward, (grad_rows, down_weight, down_mask, slopes))
    potential_grad = jnp.transpose(grads, (1, 0, 2))
    return (mixed, gate_grad, potential_grad)
```

```python
import functools
import math

import jax
import jax.numpy as jnp
from jax import lax
from jax.experimental import pallas as pl
from jax.experimental.pallas import tpu as pltpu
from jax.sharding import Mesh, PartitionSpec as P

BF = jnp.bfloat16
F32 = jnp.float32
SIDE = 128
GROUP = 4
VMEM = 56 * 1024 * 1024
PLANE = ("core", "expert")


def params():
    return pltpu.CompilerParams(vmem_limit_bytes=VMEM)


def live_part(ref, mask_ref, at, size):
    blocks = [
        ref[i * SIDE : (i + 1) * SIDE, at : at + size] * mask_ref[i, :, at : at + size].astype(BF)
        for i in range(mask_ref.shape[0])
    ]
    return jnp.concatenate(blocks, axis=0)


def forward_kernel(core_ref, *refs, pieces, chunk):
    xs = refs[:pieces]
    uo, ut, do, dt, up_mask, down_mask, scale_ref, slope_own, slope_other = refs[
        pieces : pieces + 9
    ]
    parts = refs[pieces + 9 : -4]
    up, down, hid, sems = refs[-4:]
    _, width, half = uo.shape
    core = core_ref[0]
    copies = [
        pltpu.make_async_copy(uo.at[core], up.at[:, pl.ds(0, half)], sems.at[0]),
        pltpu.make_async_copy(ut.at[core], up.at[:, pl.ds(half, half)], sems.at[1]),
        pltpu.make_async_copy(do.at[core], down.at[pl.ds(0, half), :], sems.at[2]),
        pltpu.make_async_copy(dt.at[core], down.at[pl.ds(half, half), :], sems.at[3]),
    ]
    for c in copies:
        c.start()
    scale = scale_ref[...]
    x = jnp.concatenate([r[...] for r in xs], axis=0) if pieces > 1 else xs[0][...]
    copies[0].wait()
    pending = True
    for at in range(0, 2 * half, chunk):
        if pending and at + chunk > half:
            copies[1].wait()
            pending = False
        potential = jnp.dot(x, live_part(up, up_mask, at, chunk), preferred_element_type=F32)
        sig = jax.nn.sigmoid(potential)
        by = scale[:, at : at + chunk]
        hid[:, at : at + chunk] = (potential * sig * by).astype(BF)
        slope = (sig * (1.0 + potential * (1.0 - sig)) * by).astype(BF)
        for b in range(at, at + chunk, SIDE):
            out, to = (slope_own, b) if b < half else (slope_other, b - half)
            out[:, to : to + SIDE] = slope[:, b - at : b - at + SIDE]
    copies[2].wait()
    copies[3].wait()
    tiles, rows, lanes = parts[0].shape
    per = max(1, min(chunk, width) // lanes)
    for c in range(0, tiles, per):
        live = live_part(down, down_mask, c * lanes, per * lanes)
        res = jnp.dot(hid[...], live, preferred_element_type=F32).astype(BF)
        for p, part in enumerate(parts):
            for i in range(per):
                part[c + i] = res[p * rows : (p + 1) * rows, i * lanes : (i + 1) * lanes]


def forward_rows(xs, core, ups, downs, masks, scale, parts, tiles):
    width = xs[0].shape[1]
    rows = sum(x.shape[0] for x in xs)
    hidden = ups[0].shape[2]
    lanes = width // tiles
    hbm = pl.BlockSpec(memory_space=pl.ANY)
    vmem = pl.BlockSpec(memory_space=pltpu.VMEM)
    smem = pl.BlockSpec(memory_space=pltpu.SMEM)
    return pl.pallas_call(
        functools.partial(forward_kernel, pieces=len(xs), chunk=2 * SIDE),
        in_specs=[smem] + [vmem] * len(xs) + [hbm] * 4 + [vmem] * 3,
        out_specs=[vmem] * (2 + parts),
        out_shape=[jax.ShapeDtypeStruct((rows, hidden), BF)] * 2
        + [jax.ShapeDtypeStruct((tiles, rows // parts, lanes), BF)] * parts,
        scratch_shapes=[
            pltpu.VMEM((width, 2 * hidden), BF),
            pltpu.VMEM((2 * hidden, width), BF),
            pltpu.VMEM((rows, 2 * hidden), BF),
            pltpu.SemaphoreType.DMA((4,)),
        ],
        compiler_params=params(),
        cost_estimate=pl.CostEstimate(
            flops=8 * rows * width * hidden,
            transcendentals=rows * hidden * 2,
            bytes_accessed=16 * 2**20,
        ),
        name="forward_rows",
    )(core, *xs, *ups, *downs, *masks, scale)


def backward_kernel(core_ref, g_ref, do_ref, dt_ref, mask_ref, *refs, counts):
    slopes = refs[: 2 * len(counts)]
    own_ref, other_ref, rows_ref = refs[2 * len(counts) :]
    lanes = g_ref.shape[2]
    tiles = g_ref.shape[0] // 2
    shards = sum(counts)
    block = g_ref.shape[1] // shards

    @pl.when(pl.program_id(0) == 0)
    def _():
        for s in range(shards):
            for k in range(2):
                for c in range(tiles):
                    rows_ref[
                        (s * 2 + k) * block : (s * 2 + k + 1) * block, c * lanes : (c + 1) * lanes
                    ] = g_ref[k * tiles + c, s * block : (s + 1) * block, :]

    step = pl.program_id(0)
    half = mask_ref.shape[0] // 2
    w_down = jnp.concatenate(
        [do_ref[...] * mask_ref[step].astype(BF), dt_ref[...] * mask_ref[half + step].astype(BF)],
        axis=0,
    )
    at = 0
    for i, n in enumerate(counts):
        size = n * 2 * block
        back = lax.dot_general(
            rows_ref[at : at + size, :], w_down, (((1,), (1,)), ((), ())),
            preferred_element_type=F32,
        )
        own_ref[at : at + size, :] = (back[:, :SIDE] * slopes[2 * i][...].astype(F32)).astype(BF)
        other_ref[at : at + size, :] = (
            back[:, SIDE:] * slopes[2 * i + 1][...].astype(F32)
        ).astype(BF)
        at += size


def backward_rows(g, core, downs, mask, slopes, counts):
    _, hidden, width = downs[0].shape
    rows = g.shape[1] * 2
    row = pl.BlockSpec((pl.Squeezed(), SIDE, width), lambda i, c: (c[0], i, 0))
    col = pl.BlockSpec((rows, SIDE), lambda i, c: (0, i))
    return pl.pallas_call(
        functools.partial(backward_kernel, counts=counts),
        grid_spec=pltpu.PrefetchScalarGridSpec(
            num_scalar_prefetch=1,
            grid=(hidden // SIDE,),
            in_specs=[
                pl.BlockSpec(g.shape, lambda i, c: (0, 0, 0)),
                row,
                row,
                pl.BlockSpec(mask.shape, lambda i, c: (0, 0, 0)),
            ]
            + [pl.BlockSpec((s.shape[0], SIDE), lambda i, c: (0, i)) for s in slopes],
            out_specs=[col, col],
            scratch_shapes=[pltpu.VMEM((rows, width), BF)],
        ),
        out_shape=[jax.ShapeDtypeStruct((rows, hidden), BF)] * 2,
        compiler_params=params(),
        cost_estimate=pl.CostEstimate(
            flops=4 * rows * width * hidden, transcendentals=0, bytes_accessed=24 * 2**20
        ),
        name="backward_rows",
    )(core, g, *downs, mask, *slopes)


def lanes_of(meta_ref, line):
    return jnp.concatenate([meta_ref[0, b, line : line + 1, :] for b in range(GROUP)], axis=1)


def columns_of(meta_ref):
    return jnp.concatenate([meta_ref[0, b].astype(F32).T for b in range(GROUP)], axis=0)


def grad_rows_kernel(order_ref, meta_ref, cot_ref, out_ref):
    dests, block, lanes = out_ref.shape
    rows = dests * block
    toks = cot_ref.shape[0]
    cot = cot_ref[...].astype(F32)
    cols = columns_of(meta_ref)
    place = lax.broadcasted_iota(jnp.int32, (rows, toks), 0)
    total = None
    for k in range(2):
        scaled = (cols[:, 2 + k : 3 + k] * (1.0 / 65536.0) * cot).astype(BF)
        pick = jnp.where(place == lanes_of(meta_ref, k), 1.0, 0.0).astype(BF)
        term = jnp.dot(pick, scaled, preferred_element_type=F32)
        total = term if total is None else total + term
    out_ref[...] = total.reshape(dests, block, lanes).astype(BF)


def grad_rows(order, meta, cot, dests, block):
    groups = cot.shape[0] // (GROUP * SIDE)
    per = groups // order.shape[0]
    toks = GROUP * SIDE
    lanes = cot.shape[1]
    return pl.pallas_call(
        grad_rows_kernel,
        grid_spec=pltpu.PrefetchScalarGridSpec(
            num_scalar_prefetch=1,
            grid=(groups,),
            in_specs=[
                pl.BlockSpec(
                    (1, GROUP, 8, SIDE), lambda i, o: (o[i // per] * per + i % per, 0, 0, 0)
                ),
                pl.BlockSpec((toks, lanes), lambda i, o: (i, 0)),
            ],
            out_specs=pl.BlockSpec((dests, block, lanes), lambda i, o: (0, i, 0)),
        ),
        out_shape=jax.ShapeDtypeStruct((dests, groups * block, lanes), BF),
        compiler_params=params(),
        cost_estimate=pl.CostEstimate(
            flops=groups * dests * block * toks * lanes * 8, transcendentals=0,
            bytes_accessed=10 * 2**20,
        ),
        name="grad_rows",
    )(order, meta, cot)


def combine_kernel(here_ref, meta_ref, cot_ref, back_ref, mixed_ref, gg_ref):
    dests, block, lanes = back_ref.shape
    rows = dests * block
    toks = cot_ref.shape[0]
    back = back_ref[...].reshape(rows, lanes)
    cot = cot_ref[...].astype(F32)
    cols = columns_of(meta_ref)
    place = lax.broadcasted_iota(jnp.int32, (toks, rows), 1)
    line = lax.broadcasted_iota(jnp.int32, (8, lanes), 0)
    mixed = None
    grads = None
    for k in range(2):
        pick = jnp.where(place == cols[:, k : k + 1].astype(jnp.int32), 1.0, 0.0).astype(BF)
        picked = jnp.dot(pick, back, preferred_element_type=F32)
        term = cols[:, 2 + k : 3 + k] * (1.0 / 65536.0) * picked
        mixed = term if mixed is None else mixed + term
        ones = jnp.where(line == k, 1.0, 0.0)
        part = lax.dot_general(
            ones, cot * picked, (((1,), (1,)), ((), ())),
            precision=lax.Precision.HIGHEST, preferred_element_type=F32,
        )
        grads = part if grads is None else grads + part
    mixed_ref[...] = mixed.astype(BF)
    for s in range(GROUP):
        gg_ref[s] = grads[:, s * SIDE : (s + 1) * SIDE]


def combine(here, meta, cot, back):
    dests, total, lanes = back.shape
    toks = cot.shape[0]
    sources = toks // SIDE
    groups = sources // GROUP
    return pl.pallas_call(
        combine_kernel,
        grid_spec=pltpu.PrefetchScalarGridSpec(
            num_scalar_prefetch=1,
            grid=(groups,),
            in_specs=[
                pl.BlockSpec((1, GROUP, 8, SIDE), lambda i, h: (h[0] * groups + i, 0, 0, 0)),
                pl.BlockSpec((toks // groups, lanes), lambda i, h: (i, 0)),
                pl.BlockSpec((dests, total // groups, lanes), lambda i, h: (0, i, 0)),
            ],
            out_specs=[
                pl.BlockSpec((toks // groups, lanes), lambda i, h: (i, 0)),
                pl.BlockSpec((GROUP, 8, SIDE), lambda i, h: (i, 0, 0)),
            ],
        ),
        out_shape=[
            jax.ShapeDtypeStruct((toks, lanes), BF),
            jax.ShapeDtypeStruct((sources, 8, SIDE), F32),
        ],
        compiler_params=params(),
        name="combine",
    )(here, meta, cot, back)


def pack_kernel(at_ref, own_ref, other_ref, out_ref):
    rows, _, width = out_ref.shape
    core = at_ref[0]
    line = lax.broadcasted_iota(jnp.int32, (2 * rows, 2 * rows), 0)
    lane = lax.broadcasted_iota(jnp.int32, (2 * rows, 2 * rows), 1)
    want = jnp.where(line % 2 == core, line // 2, rows + line // 2)
    order = jnp.where(lane == want, 1.0, 0.0).astype(BF)
    both = jnp.concatenate([own_ref[...], other_ref[...]], axis=0)
    mixed = jnp.dot(order, both, preferred_element_type=F32).astype(BF)
    out_ref[...] = mixed.reshape(rows, 2, width)


def pack(at, own, other, rows):
    total, width = own.shape
    per = total // (at.shape[0] - 1) // rows

    def source(i, at):
        return (at[1 + i // per] * per + i % per, 0)

    return pl.pallas_call(
        pack_kernel,
        grid_spec=pltpu.PrefetchScalarGridSpec(
            num_scalar_prefetch=1,
            grid=(total // rows,),
            in_specs=[pl.BlockSpec((rows, width), source)] * 2,
            out_specs=pl.BlockSpec((rows, 2, width), lambda i, at: (i, 0, 0)),
        ),
        out_shape=jax.ShapeDtypeStruct((total, 2, width), BF),
        compiler_params=params(),
        name="pack",
    )(at, own, other)


def after(value, *others):
    return lax.optimization_barrier((value,) + others)[0]


def shards(
    tokens, routes, gate_fixed, up_weight, up_mask, down_weight, down_mask, threshold, cotangent
):
    owners = lax.axis_size("expert")
    ring = lax.axis_size("x")
    tok_rows, width = tokens.shape
    local_experts = up_weight.shape[0]
    experts = local_experts * owners
    capacity = (tok_rows * 5 + 2 * experts - 1) // (2 * experts)
    lanes = width // owners
    core = lax.axis_index("core")
    column = lax.axis_index("expert")
    here = lax.axis_index("x")
    inv_root = 1.0 / math.sqrt(width)
    right = [(i, (i + 1) % ring) for i in range(ring)]
    left = [(i, (i - 1) % ring) for i in range(ring)]
    across = [(i, (i + 2) % ring) for i in range(ring)]
    swap = [(0, 1), (1, 0)]

    cot_r = lax.ppermute(cotangent, "x", right)
    cot_l = lax.ppermute(cotangent, "x", left)
    cot_far = lax.ppermute(cotangent, "x", across)

    by_tok = routes.T
    same = (by_tok[:, :, None, None] == by_tok[None, None]).astype(jnp.int32)
    before = jnp.arange(tok_rows)[:, None] < jnp.arange(tok_rows)[None, :]
    slot = jnp.sum(jnp.where(before[None, :, None, :], same, 0), axis=(0, 1))
    target = by_tok % local_experts * owners + by_tok // local_experts
    place = target * capacity + slot
    block = GROUP * capacity
    col = target * block + column % GROUP * capacity + slot

    meta = jnp.concatenate([col, gate_fixed.T, jnp.zeros((4, tok_rows), jnp.int32)], axis=0)
    meta = jnp.broadcast_to(meta[None], (ring * owners,) + meta.shape)
    meta = lax.all_to_all(meta, ("x", "expert"), split_axis=0, concat_axis=0, tiled=True)
    meta = meta.reshape(ring * owners // GROUP, GROUP, 8, tok_rows)
    order = (here + jnp.array([0, -1, 1, 2], jnp.int32)) % ring

    take = jnp.arange(experts * capacity, dtype=jnp.int32)[:, None]
    pick = ((take == place[0][None]) | (take == place[1][None])).astype(BF)
    sent = jnp.dot(pick, tokens, preferred_element_type=F32).astype(BF)
    sent = after(sent.reshape(experts, capacity // 2, 2, width), meta)
    arrived = lax.all_to_all(sent, PLANE, split_axis=0, concat_axis=0, tiled=True)
    x_own = lax.optimization_barrier(arrived.reshape(experts * capacity, width))
    x_r = lax.ppermute(x_own, "x", right)
    x_l = lax.ppermute(x_own, "x", left)

    ups = (up_weight, lax.ppermute(up_weight, "core", swap))
    downs = (down_weight, lax.ppermute(down_weight, "core", swap))
    small = jnp.concatenate(
        [up_mask.reshape(2, -1), down_mask.reshape(2, -1), threshold], axis=1
    )
    keep = lax.dynamic_index_in_dim(small, core, 0, keepdims=False)
    got = lax.ppermute(
        lax.dynamic_index_in_dim(small, 1 - core, 0, keepdims=False), "core", swap
    )
    n_up, n_down = up_mask[0].size, down_mask[0].size

    def piece(a):
        u = a[:n_up].reshape(up_mask.shape[1:])
        d = a[n_up : n_up + n_down].reshape(down_mask.shape[1:])
        return u, d, a[n_up + n_down :]

    pairs = [jnp.concatenate(p, axis=n) for p, n in zip(zip(piece(keep), piece(got)), (1, 0, 0))]
    masks = [jnp.repeat(p.astype(F32), SIDE, axis=1)[:, None, :] for p in pairs[:2]]
    scale = 4.0 / pairs[2].astype(F32)[None]
    core_at = core.reshape(1)

    cot_all = jnp.concatenate([cotangent, cot_r, cot_l, cot_far], axis=0)
    built = grad_rows(order, meta, after(cot_all, x_own), experts, block)
    x_r, x_l, built = lax.optimization_barrier((x_r, x_l, built))
    grads = lax.all_to_all(built, PLANE, split_axis=0, concat_axis=0, tiled=True)

    mid = x_own.shape[0] // 2
    x_rh, x_lh = x_r[:mid], x_l[mid:]
    x_rr = lax.ppermute(x_rh, "x", right)
    x_ll = lax.ppermute(x_lh, "x", left)
    run = functools.partial(
        forward_rows, core=core_at, ups=ups, downs=downs, masks=masks, scale=scale, tiles=owners
    )
    so0, st0, p0a, p0b = run([after(x_own, x_rh, x_lh)], parts=2)
    so1, st1, lefta, leftb, righta, rightb = run([after(x_r, so0), x_l], parts=4)
    so2, st2, fara, farb = run([after(x_rr, so1), x_ll], parts=2)
    r_b = lax.ppermute(rightb, "x", right)
    l_a = lax.ppermute(lefta, "x", left)
    fara, farb = lax.optimization_barrier((fara, farb, r_b, l_a))[:2]
    r_far = lax.ppermute(fara, "x", right)
    l_far = lax.ppermute(farb, "x", left)

    def add(*v):
        return sum(a.astype(F32) for a in v).astype(BF)

    r_go, l_go = lax.optimization_barrier((add(righta, r_far), add(leftb, l_far)))
    r_a = lax.ppermute(r_go, "x", right)
    l_b = lax.ppermute(l_go, "x", left)

    summed = jnp.concatenate([add(p0a, r_a, l_a), add(p0b, r_b, l_b)], axis=0)
    back = lax.all_to_all(summed, PLANE, split_axis=0, concat_axis=0, tiled=True)

    slopes = (so0, st0, so1, st1, so2, st2)
    own, other = backward_rows(
        after(grads, r_go, l_go), core_at, downs, masks[1], slopes, (1, 2, 1)
    )
    other = lax.ppermute(other, "core", swap)

    mixed, gg = combine(here.reshape(1), meta, cotangent, after(back, own))
    gg_all = lax.all_to_all(gg, "expert", split_axis=0, concat_axis=0, tiled=True)
    from_shard = jnp.array([0, 2, 3, 1], jnp.int32)[(jnp.arange(ring) - here) % ring]
    at = jnp.concatenate([core.reshape(1), from_shard]).astype(jnp.int32)
    potential_grad = pack(at, after(own, gg), other, x_own.shape[0] // 2)
    gg_all = after(gg_all, potential_grad)
    gate_grad = (jnp.sum(gg_all, axis=0)[:2] * inv_root).T
    return (mixed, gate_grad, potential_grad)


def solution(mesh):
    devices = mesh.devices
    split = Mesh(
        devices.reshape(devices.shape[0] // 2, 2, devices.shape[1]), ("x", "core", "expert")
    )
    dp = ("x", "core")
    every = ("x", "core", "expert")
    placed = (
        P(every, None),
        P(every, None),
        P(every, None),
        P("expert", None, dp),
        P("expert", None, dp),
        P("expert", dp, None),
        P("expert", dp, None),
        P("expert", dp),
        P(dp, "expert"),
    )
    return jax.shard_map(
        shards,
        mesh=split,
        in_specs=placed,
        out_specs=(P(dp, "expert"), P(every, None), P(None, "expert", dp)),
        check_vma=False,
    )
```

```python
import functools
import math

import jax
import jax.numpy as jnp
from jax import lax
from jax.experimental import pallas as pl
from jax.experimental.pallas import tpu as pltpu
from jax.sharding import Mesh, PartitionSpec as P

BF = jnp.bfloat16
F32 = jnp.float32
SIDE = 128
GROUP = 4
VMEM = 56 * 1024 * 1024
PLANE = ("core", "expert")


def params():
    return pltpu.CompilerParams(vmem_limit_bytes=VMEM)


def live_part(ref, mask_ref, at, size):
    blocks = [
        ref[i * SIDE : (i + 1) * SIDE, at : at + size] * mask_ref[i, :, at : at + size].astype(BF)
        for i in range(mask_ref.shape[0])
    ]
    return jnp.concatenate(blocks, axis=0)


def forward_kernel(core_ref, *refs, pieces, chunk):
    xs = refs[:pieces]
    uo, ut, do, dt, up_mask, down_mask, scale_ref, slope_own, slope_other = refs[
        pieces : pieces + 9
    ]
    parts = refs[pieces + 9 : -4]
    up, down, hid, sems = refs[-4:]
    _, width, half = uo.shape
    core = core_ref[0]
    copies = [
        pltpu.make_async_copy(uo.at[core], up.at[:, pl.ds(0, half)], sems.at[0]),
        pltpu.make_async_copy(ut.at[core], up.at[:, pl.ds(half, half)], sems.at[1]),
        pltpu.make_async_copy(do.at[core], down.at[pl.ds(0, half), :], sems.at[2]),
        pltpu.make_async_copy(dt.at[core], down.at[pl.ds(half, half), :], sems.at[3]),
    ]
    for c in copies:
        c.start()
    scale = scale_ref[...]
    x = jnp.concatenate([r[...] for r in xs], axis=0) if pieces > 1 else xs[0][...]
    copies[0].wait()
    pending = True
    for at in range(0, 2 * half, chunk):
        if pending and at + chunk > half:
            copies[1].wait()
            pending = False
        potential = jnp.dot(x, live_part(up, up_mask, at, chunk), preferred_element_type=F32)
        sig = jax.nn.sigmoid(potential)
        by = scale[:, at : at + chunk]
        hid[:, at : at + chunk] = (potential * sig * by).astype(BF)
        slope = (sig * (1.0 + potential * (1.0 - sig)) * by).astype(BF)
        for b in range(at, at + chunk, SIDE):
            out, to = (slope_own, b) if b < half else (slope_other, b - half)
            out[:, to : to + SIDE] = slope[:, b - at : b - at + SIDE]
    copies[2].wait()
    copies[3].wait()
    tiles, rows, lanes = parts[0].shape
    per = max(1, min(chunk, width) // lanes)
    for c in range(0, tiles, per):
        live = live_part(down, down_mask, c * lanes, per * lanes)
        res = jnp.dot(hid[...], live, preferred_element_type=F32).astype(BF)
        for p, part in enumerate(parts):
            for i in range(per):
                part[c + i] = res[p * rows : (p + 1) * rows, i * lanes : (i + 1) * lanes]


def forward_rows(xs, core, ups, downs, masks, scale, parts, tiles):
    width = xs[0].shape[1]
    rows = sum(x.shape[0] for x in xs)
    hidden = ups[0].shape[2]
    lanes = width // tiles
    hbm = pl.BlockSpec(memory_space=pl.ANY)
    vmem = pl.BlockSpec(memory_space=pltpu.VMEM)
    smem = pl.BlockSpec(memory_space=pltpu.SMEM)
    return pl.pallas_call(
        functools.partial(forward_kernel, pieces=len(xs), chunk=2 * SIDE),
        in_specs=[smem] + [vmem] * len(xs) + [hbm] * 4 + [vmem] * 3,
        out_specs=[vmem] * (2 + parts),
        out_shape=[jax.ShapeDtypeStruct((rows, hidden), BF)] * 2
        + [jax.ShapeDtypeStruct((tiles, rows // parts, lanes), BF)] * parts,
        scratch_shapes=[
            pltpu.VMEM((width, 2 * hidden), BF),
            pltpu.VMEM((2 * hidden, width), BF),
            pltpu.VMEM((rows, 2 * hidden), BF),
            pltpu.SemaphoreType.DMA((4,)),
        ],
        compiler_params=params(),
        cost_estimate=pl.CostEstimate(
            flops=8 * rows * width * hidden,
            transcendentals=rows * hidden * 2,
            bytes_accessed=16 * 2**20,
        ),
        name="forward_rows",
    )(core, *xs, *ups, *downs, *masks, scale)


def backward_kernel(core_ref, g_ref, do_ref, dt_ref, mask_ref, *refs, counts):
    slopes = refs[: 2 * len(counts)]
    own_ref, other_ref, rows_ref = refs[2 * len(counts) :]
    lanes = g_ref.shape[2]
    tiles = g_ref.shape[0] // 2
    shards = sum(counts)
    block = g_ref.shape[1] // shards

    @pl.when(pl.program_id(0) == 0)
    def _():
        for s in range(shards):
            for k in range(2):
                for c in range(tiles):
                    rows_ref[
                        (s * 2 + k) * block : (s * 2 + k + 1) * block, c * lanes : (c + 1) * lanes
                    ] = g_ref[k * tiles + c, s * block : (s + 1) * block, :]

    step = pl.program_id(0)
    half = mask_ref.shape[0] // 2
    w_down = jnp.concatenate(
        [do_ref[...] * mask_ref[step].astype(BF), dt_ref[...] * mask_ref[half + step].astype(BF)],
        axis=0,
    )
    at = 0
    for i, n in enumerate(counts):
        size = n * 2 * block
        back = lax.dot_general(
            rows_ref[at : at + size, :], w_down, (((1,), (1,)), ((), ())),
            preferred_element_type=F32,
        )
        own_ref[at : at + size, :] = (back[:, :SIDE] * slopes[2 * i][...].astype(F32)).astype(BF)
        other_ref[at : at + size, :] = (
            back[:, SIDE:] * slopes[2 * i + 1][...].astype(F32)
        ).astype(BF)
        at += size


def backward_rows(g, core, downs, mask, slopes, counts):
    _, hidden, width = downs[0].shape
    rows = g.shape[1] * 2
    row = pl.BlockSpec((pl.Squeezed(), SIDE, width), lambda i, c: (c[0], i, 0))
    col = pl.BlockSpec((rows, SIDE), lambda i, c: (0, i))
    return pl.pallas_call(
        functools.partial(backward_kernel, counts=counts),
        grid_spec=pltpu.PrefetchScalarGridSpec(
            num_scalar_prefetch=1,
            grid=(hidden // SIDE,),
            in_specs=[
                pl.BlockSpec(g.shape, lambda i, c: (0, 0, 0)),
                row,
                row,
                pl.BlockSpec(mask.shape, lambda i, c: (0, 0, 0)),
            ]
            + [pl.BlockSpec((s.shape[0], SIDE), lambda i, c: (0, i)) for s in slopes],
            out_specs=[col, col],
            scratch_shapes=[pltpu.VMEM((rows, width), BF)],
        ),
        out_shape=[jax.ShapeDtypeStruct((rows, hidden), BF)] * 2,
        compiler_params=params(),
        cost_estimate=pl.CostEstimate(
            flops=4 * rows * width * hidden, transcendentals=0, bytes_accessed=24 * 2**20
        ),
        name="backward_rows",
    )(core, g, *downs, mask, *slopes)


def sources_of(piece, block):
    slots = block // GROUP
    return range(piece * 8 // slots, (piece * 8 + 7) // slots + 1)


def columns_of(meta_ref):
    return jnp.concatenate([meta_ref[b, 0].astype(F32).T for b in range(GROUP)], axis=0)


def grad_rows_kernel(meta_ref, cot_ref, out_ref):
    dests, block, lanes = out_ref.shape
    cot = cot_ref[...].astype(F32)
    cols = columns_of(meta_ref)
    scaled = [(cols[:, 2 + k : 3 + k] * (1.0 / 65536.0) * cot).astype(BF) for k in range(2)]
    shape = (dests, 8, SIDE)
    base = lax.broadcasted_iota(jnp.int32, shape, 0) * block + lax.broadcasted_iota(
        jnp.int32, shape, 1
    )
    out = []
    for j in range(block // 8):
        picks, values = [], []
        for b in sources_of(j, block):
            for k in range(2):
                want = meta_ref[b, 0, k : k + 1, :].reshape(1, 1, SIDE) - 8 * j
                pick = jnp.where(base == want, 1.0, 0.0)
                picks.append(pick.reshape(dests * 8, SIDE).astype(BF))
                values.append(scaled[k][b * SIDE : (b + 1) * SIDE])
        res = jnp.dot(
            jnp.concatenate(picks, axis=1), jnp.concatenate(values, axis=0),
            preferred_element_type=F32,
        )
        out.append(res.reshape(dests, 8, lanes))
    out_ref[...] = jnp.concatenate(out, axis=1).astype(BF)


def grad_rows(meta, cot, dests, block):
    groups = cot.shape[0] // (GROUP * SIDE)
    per = meta.shape[0] // GROUP
    toks = GROUP * SIDE
    lanes = cot.shape[1]
    return pl.pallas_call(
        grad_rows_kernel,
        grid=(groups,),
        in_specs=[
            pl.BlockSpec((GROUP, 1, 8, SIDE), lambda i: (i % per, i // per, 0, 0)),
            pl.BlockSpec((toks, lanes), lambda i: (i, 0)),
        ],
        out_specs=pl.BlockSpec((dests, block, lanes), lambda i: (0, i, 0)),
        out_shape=jax.ShapeDtypeStruct((dests, groups * block, lanes), BF),
        compiler_params=params(),
        cost_estimate=pl.CostEstimate(
            flops=groups * dests * block * toks * lanes * 8, transcendentals=0,
            bytes_accessed=10 * 2**20,
        ),
        name="grad_rows",
    )(meta, cot)


def combine_kernel(meta_ref, cot_ref, back_ref, mixed_ref, gg_ref):
    dests, block, lanes = back_ref.shape
    back = back_ref[...].astype(F32)
    pieces = [
        back[:, 8 * j : 8 * j + 8, :].reshape(dests * 8, lanes).astype(BF)
        for j in range(block // 8)
    ]
    at = lax.broadcasted_iota(jnp.int32, (SIDE, dests * 8), 1)
    at = at // 8 * block + at % 8
    line = lax.broadcasted_iota(jnp.int32, (8, lanes), 0)
    for b in range(GROUP):
        used = [j for j in range(block // 8) if b in sources_of(j, block)]
        values = jnp.concatenate([pieces[j] for j in used], axis=0)
        place = jnp.concatenate([at + 8 * j for j in used], axis=1)
        cot = cot_ref[b * SIDE : (b + 1) * SIDE, :].astype(F32)
        cols = meta_ref[b, 0].astype(F32).T
        mixed = None
        grads = None
        for k in range(2):
            pick = jnp.where(place == cols[:, k : k + 1].astype(jnp.int32), 1.0, 0.0).astype(BF)
            picked = jnp.dot(pick, values, preferred_element_type=F32)
            term = cols[:, 2 + k : 3 + k] * (1.0 / 65536.0) * picked
            mixed = term if mixed is None else mixed + term
            ones = jnp.where(line == k, 1.0, 0.0)
            part = lax.dot_general(
                ones, cot * picked, (((1,), (1,)), ((), ())),
                precision=lax.Precision.HIGHEST, preferred_element_type=F32,
            )
            grads = part if grads is None else grads + part
        mixed_ref[b * SIDE : (b + 1) * SIDE, :] = mixed.astype(BF)
        gg_ref[b] = grads


def combine(meta, cot, back):
    dests, total, lanes = back.shape
    toks = cot.shape[0]
    sources = toks // SIDE
    groups = sources // GROUP
    return pl.pallas_call(
        combine_kernel,
        grid=(groups,),
        in_specs=[
            pl.BlockSpec((GROUP, 1, 8, SIDE), lambda i: (i, 0, 0, 0)),
            pl.BlockSpec((toks // groups, lanes), lambda i: (i, 0)),
            pl.BlockSpec((dests, total // groups, lanes), lambda i: (0, i, 0)),
        ],
        out_specs=[
            pl.BlockSpec((toks // groups, lanes), lambda i: (i, 0)),
            pl.BlockSpec((GROUP, 8, SIDE), lambda i: (i, 0, 0)),
        ],
        out_shape=[
            jax.ShapeDtypeStruct((toks, lanes), BF),
            jax.ShapeDtypeStruct((sources, 8, SIDE), F32),
        ],
        compiler_params=params(),
        name="combine",
    )(meta, cot, back)


def pack_kernel(at_ref, own_ref, other_ref, out_ref):
    rows, _, width = out_ref.shape
    core = at_ref[0]
    line = lax.broadcasted_iota(jnp.int32, (2 * rows, 2 * rows), 0)
    lane = lax.broadcasted_iota(jnp.int32, (2 * rows, 2 * rows), 1)
    want = jnp.where(line % 2 == core, line // 2, rows + line // 2)
    order = jnp.where(lane == want, 1.0, 0.0).astype(BF)
    both = jnp.concatenate([own_ref[...], other_ref[...]], axis=0)
    mixed = jnp.dot(order, both, preferred_element_type=F32).astype(BF)
    out_ref[...] = mixed.reshape(rows, 2, width)


def pack(at, own, other, rows):
    total, width = own.shape
    per = total // (at.shape[0] - 1) // rows

    def source(i, at):
        return (at[1 + i // per] * per + i % per, 0)

    return pl.pallas_call(
        pack_kernel,
        grid_spec=pltpu.PrefetchScalarGridSpec(
            num_scalar_prefetch=1,
            grid=(total // rows,),
            in_specs=[pl.BlockSpec((rows, width), source)] * 2,
            out_specs=pl.BlockSpec((rows, 2, width), lambda i, at: (i, 0, 0)),
        ),
        out_shape=jax.ShapeDtypeStruct((total, 2, width), BF),
        compiler_params=params(),
        name="pack",
    )(at, own, other)


def after(value, *others):
    return lax.optimization_barrier((value,) + others)[0]


def shards(
    tokens, routes, gate_fixed, up_weight, up_mask, down_weight, down_mask, threshold, cotangent
):
    owners = lax.axis_size("expert")
    ring = lax.axis_size("x")
    tok_rows, width = tokens.shape
    local_experts = up_weight.shape[0]
    experts = local_experts * owners
    capacity = (tok_rows * 5 + 2 * experts - 1) // (2 * experts)
    lanes = width // owners
    core = lax.axis_index("core")
    column = lax.axis_index("expert")
    here = lax.axis_index("x")
    inv_root = 1.0 / math.sqrt(width)
    right = [(i, (i + 1) % ring) for i in range(ring)]
    left = [(i, (i - 1) % ring) for i in range(ring)]
    across = [(i, (i + 2) % ring) for i in range(ring)]
    swap = [(0, 1), (1, 0)]

    cot_r = lax.ppermute(cotangent, "x", right)
    cot_l = lax.ppermute(cotangent, "x", left)
    mid = cotangent.shape[0] // 2
    cot_rr = lax.ppermute(cot_r[:mid], "x", right)
    cot_ll = lax.ppermute(cot_l[mid:], "x", left)

    by_tok = routes.T
    same = (by_tok[:, :, None, None] == by_tok[None, None]).astype(jnp.int32)
    before = jnp.arange(tok_rows)[:, None] < jnp.arange(tok_rows)[None, :]
    slot = jnp.sum(jnp.where(before[None, :, None, :], same, 0), axis=(0, 1))
    target = by_tok % local_experts * owners + by_tok // local_experts
    place = target * capacity + slot
    block = GROUP * capacity
    col = target * block + column % GROUP * capacity + slot

    meta = jnp.concatenate([col, gate_fixed.T, jnp.zeros((4, tok_rows), jnp.int32)], axis=0)
    meta = [meta] + [lax.ppermute(meta, "x", to) for to in (right, left, across)]
    meta = jnp.stack(meta, axis=0)

    take = jnp.arange(experts * capacity, dtype=jnp.int32)[:, None]
    pick = ((take == place[0][None]) | (take == place[1][None])).astype(BF)
    sent = jnp.dot(pick, tokens, preferred_element_type=F32).astype(BF)
    sent = sent.reshape(experts, capacity // 2, 2, width)
    arrived = lax.all_to_all(sent, PLANE, split_axis=0, concat_axis=0, tiled=True)
    ups = (up_weight, lax.ppermute(up_weight, "core", swap))
    downs = (down_weight, lax.ppermute(down_weight, "core", swap))
    small = jnp.concatenate(
        [up_mask.reshape(2, -1), down_mask.reshape(2, -1), threshold], axis=1
    )
    keep = lax.dynamic_index_in_dim(small, core, 0, keepdims=False)
    got = lax.ppermute(
        lax.dynamic_index_in_dim(small, 1 - core, 0, keepdims=False), "core", swap
    )
    n_up, n_down = up_mask[0].size, down_mask[0].size

    def piece(a):
        u = a[:n_up].reshape(up_mask.shape[1:])
        d = a[n_up : n_up + n_down].reshape(down_mask.shape[1:])
        return u, d, a[n_up + n_down :]

    pairs = [jnp.concatenate(p, axis=n) for p, n in zip(zip(piece(keep), piece(got)), (1, 0, 0))]
    masks = [jnp.repeat(p.astype(F32), SIDE, axis=1)[:, None, :] for p in pairs[:2]]
    scale = 4.0 / pairs[2].astype(F32)[None]
    core_at = core.reshape(1)

    x_own, masks, scale, cot_rr, cot_ll, meta = lax.optimization_barrier(
        (arrived.reshape(experts * capacity, width), masks, scale, cot_rr, cot_ll, meta)
    )
    x_r = lax.ppermute(x_own, "x", right)
    x_l = lax.ppermute(x_own, "x", left)

    meta = jnp.broadcast_to(after(meta, x_own)[None], (owners,) + meta.shape)
    meta = lax.all_to_all(meta, "expert", split_axis=0, concat_axis=0, tiled=True)

    cot_all = jnp.concatenate([cotangent, cot_r, cot_l, cot_rr, cot_ll], axis=0)
    built = grad_rows(meta, after(cot_all, x_own), experts, block)
    x_r, x_l, built = lax.optimization_barrier((x_r, x_l, built))
    grads = lax.all_to_all(built, PLANE, split_axis=0, concat_axis=0, tiled=True)

    mid = x_own.shape[0] // 2
    x_rh, x_lh = x_r[:mid], x_l[mid:]
    x_rr = lax.ppermute(x_rh, "x", right)
    x_ll = lax.ppermute(x_lh, "x", left)
    run = functools.partial(
        forward_rows, core=core_at, ups=ups, downs=downs, masks=masks, scale=scale, tiles=owners
    )
    so0, st0, p0a, p0b = run([after(x_own, x_rh, x_lh)], parts=2)
    so1, st1, lefta, leftb, righta, rightb = run([after(x_r, so0), x_l], parts=4)
    so2, st2, fara, farb = run([after(x_rr, so1), x_ll], parts=2)
    r_b = lax.ppermute(rightb, "x", right)
    l_a = lax.ppermute(lefta, "x", left)
    fara, farb = lax.optimization_barrier((fara, farb, r_b, l_a))[:2]
    r_far = lax.ppermute(fara, "x", right)
    l_far = lax.ppermute(farb, "x", left)

    def add(*v):
        return sum(a.astype(F32) for a in v).astype(BF)

    r_go, l_go = lax.optimization_barrier((add(righta, r_far), add(leftb, l_far)))
    r_a = lax.ppermute(r_go, "x", right)
    l_b = lax.ppermute(l_go, "x", left)

    summed = jnp.concatenate([add(p0a, r_a, l_a), add(p0b, r_b, l_b)], axis=0)
    back = lax.all_to_all(summed, PLANE, split_axis=0, concat_axis=0, tiled=True)

    slopes = (so0, st0, so1, st1, so2, st2)
    own, other = backward_rows(
        after(grads, r_go, l_go), core_at, downs, masks[1], slopes, (1, 2, 1)
    )
    other = lax.ppermute(other, "core", swap)

    mixed, gg = combine(meta, cotangent, after(back, own))
    gg_all = lax.all_to_all(gg, "expert", split_axis=0, concat_axis=0, tiled=True)
    from_shard = jnp.array([0, 2, 3, 1], jnp.int32)[(jnp.arange(ring) - here) % ring]
    at = jnp.concatenate([core.reshape(1), from_shard]).astype(jnp.int32)
    potential_grad = pack(at, after(own, gg), other, x_own.shape[0] // 2)
    gg_all = after(gg_all, potential_grad)
    gate_grad = (jnp.sum(gg_all, axis=0)[:2] * inv_root).T
    return (mixed, gate_grad, potential_grad)


def solution(mesh):
    devices = mesh.devices
    split = Mesh(
        devices.reshape(devices.shape[0] // 2, 2, devices.shape[1]), ("x", "core", "expert")
    )
    dp = ("x", "core")
    every = ("x", "core", "expert")
    placed = (
        P(every, None),
        P(every, None),
        P(every, None),
        P("expert", None, dp),
        P("expert", None, dp),
        P("expert", dp, None),
        P("expert", dp, None),
        P("expert", dp),
        P(dp, "expert"),
    )
    return jax.shard_map(
        shards,
        mesh=split,
        in_specs=placed,
        out_specs=(P(dp, "expert"), P(every, None), P(None, "expert", dp)),
        check_vma=False,
    )
```

```python
import functools
import math

import jax
import jax.numpy as jnp
from jax import lax
from jax.experimental import pallas as pl
from jax.experimental.pallas import tpu as pltpu
from jax.sharding import Mesh, PartitionSpec as P

BF = jnp.bfloat16
F32 = jnp.float32
SIDE = 128
GROUP = 4
VMEM = 56 * 1024 * 1024
PLANE = ("core", "expert")


def params():
    return pltpu.CompilerParams(vmem_limit_bytes=VMEM)


def live_part(ref, mask_ref, at, size):
    blocks = [
        ref[i * SIDE : (i + 1) * SIDE, at : at + size] * mask_ref[i, :, at : at + size].astype(BF)
        for i in range(mask_ref.shape[0])
    ]
    return jnp.concatenate(blocks, axis=0)


def forward_kernel(core_ref, *refs, pieces, chunk):
    xs = refs[:pieces]
    uo, ut, do, dt, up_mask, down_mask, scale_ref, slope_own, slope_other = refs[
        pieces : pieces + 9
    ]
    parts = refs[pieces + 9 : -4]
    up, down, hid, sems = refs[-4:]
    _, width, half = uo.shape
    core = core_ref[0]
    copies = [
        pltpu.make_async_copy(uo.at[core], up.at[:, pl.ds(0, half)], sems.at[0]),
        pltpu.make_async_copy(ut.at[core], up.at[:, pl.ds(half, half)], sems.at[1]),
        pltpu.make_async_copy(do.at[core], down.at[pl.ds(0, half), :], sems.at[2]),
        pltpu.make_async_copy(dt.at[core], down.at[pl.ds(half, half), :], sems.at[3]),
    ]
    for c in copies:
        c.start()
    scale = scale_ref[...]
    x = jnp.concatenate([r[...] for r in xs], axis=0) if pieces > 1 else xs[0][...]
    copies[0].wait()
    pending = True
    for at in range(0, 2 * half, chunk):
        if pending and at + chunk > half:
            copies[1].wait()
            pending = False
        potential = jnp.dot(x, live_part(up, up_mask, at, chunk), preferred_element_type=F32)
        sig = jax.nn.sigmoid(potential)
        by = scale[:, at : at + chunk]
        hid[:, at : at + chunk] = (potential * sig * by).astype(BF)
        slope = (sig * (1.0 + potential * (1.0 - sig)) * by).astype(BF)
        for b in range(at, at + chunk, SIDE):
            out, to = (slope_own, b) if b < half else (slope_other, b - half)
            out[:, to : to + SIDE] = slope[:, b - at : b - at + SIDE]
    copies[2].wait()
    copies[3].wait()
    tiles, rows, lanes = parts[0].shape
    per = max(1, min(chunk, width) // lanes)

    def columns(c, carry):
        at = pl.multiple_of(c * per * lanes, per * lanes)
        live = jnp.concatenate(
            [
                down[i * SIDE : (i + 1) * SIDE, pl.ds(at, per * lanes)]
                * down_mask[i, :, pl.ds(at, per * lanes)].astype(BF)
                for i in range(down_mask.shape[0])
            ],
            axis=0,
        )
        res = jnp.dot(hid[...], live, preferred_element_type=F32).astype(BF)
        for p, part in enumerate(parts):
            for i in range(per):
                part[c * per + i] = res[p * rows : (p + 1) * rows, i * lanes : (i + 1) * lanes]
        return carry

    lax.fori_loop(0, tiles // per, columns, 0)


def forward_rows(xs, core, ups, downs, masks, scale, parts, tiles):
    width = xs[0].shape[1]
    rows = sum(x.shape[0] for x in xs)
    hidden = ups[0].shape[2]
    lanes = width // tiles
    hbm = pl.BlockSpec(memory_space=pl.ANY)
    vmem = pl.BlockSpec(memory_space=pltpu.VMEM)
    smem = pl.BlockSpec(memory_space=pltpu.SMEM)
    return pl.pallas_call(
        functools.partial(forward_kernel, pieces=len(xs), chunk=2 * SIDE),
        in_specs=[smem] + [vmem] * len(xs) + [hbm] * 4 + [vmem] * 3,
        out_specs=[vmem] * (2 + parts),
        out_shape=[jax.ShapeDtypeStruct((rows, hidden), BF)] * 2
        + [jax.ShapeDtypeStruct((tiles, rows // parts, lanes), BF)] * parts,
        scratch_shapes=[
            pltpu.VMEM((width, 2 * hidden), BF),
            pltpu.VMEM((2 * hidden, width), BF),
            pltpu.VMEM((rows, 2 * hidden), BF),
            pltpu.SemaphoreType.DMA((4,)),
        ],
        compiler_params=params(),
        cost_estimate=pl.CostEstimate(
            flops=8 * rows * width * hidden,
            transcendentals=rows * hidden * 2,
            bytes_accessed=16 * 2**20,
        ),
        name="forward_rows",
    )(core, *xs, *ups, *downs, *masks, scale)


def backward_kernel(core_ref, g_ref, do_ref, dt_ref, mask_ref, *refs, counts):
    slopes = refs[: 2 * len(counts)]
    own_ref, other_ref, rows_ref = refs[2 * len(counts) :]
    lanes = g_ref.shape[2]
    tiles = g_ref.shape[0] // 2
    shards = sum(counts)
    block = g_ref.shape[1] // shards

    @pl.when(pl.program_id(0) == 0)
    def _():
        for s in range(shards):
            for k in range(2):
                for c in range(tiles):
                    rows_ref[
                        (s * 2 + k) * block : (s * 2 + k + 1) * block, c * lanes : (c + 1) * lanes
                    ] = g_ref[k * tiles + c, s * block : (s + 1) * block, :]

    step = pl.program_id(0)
    half = mask_ref.shape[0] // 2
    w_down = jnp.concatenate(
        [do_ref[...] * mask_ref[step].astype(BF), dt_ref[...] * mask_ref[half + step].astype(BF)],
        axis=0,
    )
    at = 0
    for i, n in enumerate(counts):
        size = n * 2 * block
        back = lax.dot_general(
            rows_ref[at : at + size, :], w_down, (((1,), (1,)), ((), ())),
            preferred_element_type=F32,
        )
        own_ref[at : at + size, :] = (back[:, :SIDE] * slopes[2 * i][...].astype(F32)).astype(BF)
        other_ref[at : at + size, :] = (
            back[:, SIDE:] * slopes[2 * i + 1][...].astype(F32)
        ).astype(BF)
        at += size


def backward_rows(g, core, downs, mask, slopes, counts):
    _, hidden, width = downs[0].shape
    rows = g.shape[1] * 2
    row = pl.BlockSpec((pl.Squeezed(), SIDE, width), lambda i, c: (c[0], i, 0))
    col = pl.BlockSpec((rows, SIDE), lambda i, c: (0, i))
    return pl.pallas_call(
        functools.partial(backward_kernel, counts=counts),
        grid_spec=pltpu.PrefetchScalarGridSpec(
            num_scalar_prefetch=1,
            grid=(hidden // SIDE,),
            in_specs=[
                pl.BlockSpec(g.shape, lambda i, c: (0, 0, 0)),
                row,
                row,
                pl.BlockSpec(mask.shape, lambda i, c: (0, 0, 0)),
            ]
            + [pl.BlockSpec((s.shape[0], SIDE), lambda i, c: (0, i)) for s in slopes],
            out_specs=[col, col],
            scratch_shapes=[pltpu.VMEM((rows, width), BF)],
        ),
        out_shape=[jax.ShapeDtypeStruct((rows, hidden), BF)] * 2,
        compiler_params=params(),
        cost_estimate=pl.CostEstimate(
            flops=4 * rows * width * hidden, transcendentals=0, bytes_accessed=24 * 2**20
        ),
        name="backward_rows",
    )(core, g, *downs, mask, *slopes)


def sources_of(piece, block):
    slots = block // GROUP
    return range(piece * 8 // slots, (piece * 8 + 7) // slots + 1)


def columns_of(meta_ref):
    return jnp.concatenate([meta_ref[b, 0].astype(F32).T for b in range(GROUP)], axis=0)


def grad_rows_kernel(meta_ref, cot_ref, out_ref):
    dests, block, lanes = out_ref.shape
    cot = cot_ref[...].astype(F32)
    cols = columns_of(meta_ref)
    scaled = [(cols[:, 2 + k : 3 + k] * (1.0 / 65536.0) * cot).astype(BF) for k in range(2)]
    shape = (dests, 8, SIDE)
    base = lax.broadcasted_iota(jnp.int32, shape, 0) * block + lax.broadcasted_iota(
        jnp.int32, shape, 1
    )
    out = []
    for j in range(block // 8):
        picks, values = [], []
        for b in sources_of(j, block):
            for k in range(2):
                want = meta_ref[b, 0, k : k + 1, :].reshape(1, 1, SIDE) - 8 * j
                pick = jnp.where(base == want, 1.0, 0.0)
                picks.append(pick.reshape(dests * 8, SIDE).astype(BF))
                values.append(scaled[k][b * SIDE : (b + 1) * SIDE])
        res = jnp.dot(
            jnp.concatenate(picks, axis=1), jnp.concatenate(values, axis=0),
            preferred_element_type=F32,
        )
        out.append(res.reshape(dests, 8, lanes))
    out_ref[...] = jnp.concatenate(out, axis=1).astype(BF)


def grad_rows(meta, cot, dests, block):
    groups = cot.shape[0] // (GROUP * SIDE)
    per = meta.shape[0] // GROUP
    toks = GROUP * SIDE
    lanes = cot.shape[1]
    return pl.pallas_call(
        grad_rows_kernel,
        grid=(groups,),
        in_specs=[
            pl.BlockSpec((GROUP, 1, 8, SIDE), lambda i: (i % per, i // per, 0, 0)),
            pl.BlockSpec((toks, lanes), lambda i: (i, 0)),
        ],
        out_specs=pl.BlockSpec((dests, block, lanes), lambda i: (0, i, 0)),
        out_shape=jax.ShapeDtypeStruct((dests, groups * block, lanes), BF),
        compiler_params=params(),
        cost_estimate=pl.CostEstimate(
            flops=groups * dests * block * toks * lanes * 8, transcendentals=0,
            bytes_accessed=10 * 2**20,
        ),
        name="grad_rows",
    )(meta, cot)


def combine_kernel(meta_ref, cot_ref, back_ref, mixed_ref, gg_ref):
    dests, block, lanes = back_ref.shape
    back = back_ref[...].astype(F32)
    pieces = [
        back[:, 8 * j : 8 * j + 8, :].reshape(dests * 8, lanes).astype(BF)
        for j in range(block // 8)
    ]
    at = lax.broadcasted_iota(jnp.int32, (SIDE, dests * 8), 1)
    at = at // 8 * block + at % 8
    line = lax.broadcasted_iota(jnp.int32, (8, lanes), 0)
    for b in range(GROUP):
        used = [j for j in range(block // 8) if b in sources_of(j, block)]
        values = jnp.concatenate([pieces[j] for j in used], axis=0)
        place = jnp.concatenate([at + 8 * j for j in used], axis=1)
        cot = cot_ref[b * SIDE : (b + 1) * SIDE, :].astype(F32)
        cols = meta_ref[b, 0].astype(F32).T
        mixed = None
        grads = None
        for k in range(2):
            pick = jnp.where(place == cols[:, k : k + 1].astype(jnp.int32), 1.0, 0.0).astype(BF)
            picked = jnp.dot(pick, values, preferred_element_type=F32)
            term = cols[:, 2 + k : 3 + k] * (1.0 / 65536.0) * picked
            mixed = term if mixed is None else mixed + term
            ones = jnp.where(line == k, 1.0, 0.0)
            part = lax.dot_general(
                ones, cot * picked, (((1,), (1,)), ((), ())),
                precision=lax.Precision.HIGHEST, preferred_element_type=F32,
            )
            grads = part if grads is None else grads + part
        mixed_ref[b * SIDE : (b + 1) * SIDE, :] = mixed.astype(BF)
        gg_ref[b] = grads


def combine(meta, cot, back):
    dests, total, lanes = back.shape
    toks = cot.shape[0]
    sources = toks // SIDE
    groups = sources // GROUP
    return pl.pallas_call(
        combine_kernel,
        grid=(groups,),
        in_specs=[
            pl.BlockSpec((GROUP, 1, 8, SIDE), lambda i: (i, 0, 0, 0)),
            pl.BlockSpec((toks // groups, lanes), lambda i: (i, 0)),
            pl.BlockSpec((dests, total // groups, lanes), lambda i: (0, i, 0)),
        ],
        out_specs=[
            pl.BlockSpec((toks // groups, lanes), lambda i: (i, 0)),
            pl.BlockSpec((GROUP, 8, SIDE), lambda i: (i, 0, 0)),
        ],
        out_shape=[
            jax.ShapeDtypeStruct((toks, lanes), BF),
            jax.ShapeDtypeStruct((sources, 8, SIDE), F32),
        ],
        compiler_params=params(),
        name="combine",
    )(meta, cot, back)


def pack_kernel(at_ref, own_ref, other_ref, out_ref):
    rows, _, width = out_ref.shape
    core = at_ref[0]
    line = lax.broadcasted_iota(jnp.int32, (2 * rows, 2 * rows), 0)
    lane = lax.broadcasted_iota(jnp.int32, (2 * rows, 2 * rows), 1)
    want = jnp.where(line % 2 == core, line // 2, rows + line // 2)
    order = jnp.where(lane == want, 1.0, 0.0).astype(BF)
    both = jnp.concatenate([own_ref[...], other_ref[...]], axis=0)
    mixed = jnp.dot(order, both, preferred_element_type=F32).astype(BF)
    out_ref[...] = mixed.reshape(rows, 2, width)


def pack(at, own, other, rows):
    total, width = own.shape
    per = total // (at.shape[0] - 1) // rows

    def source(i, at):
        return (at[1 + i // per] * per + i % per, 0)

    return pl.pallas_call(
        pack_kernel,
        grid_spec=pltpu.PrefetchScalarGridSpec(
            num_scalar_prefetch=1,
            grid=(total // rows,),
            in_specs=[pl.BlockSpec((rows, width), source)] * 2,
            out_specs=pl.BlockSpec((rows, 2, width), lambda i, at: (i, 0, 0)),
        ),
        out_shape=jax.ShapeDtypeStruct((total, 2, width), BF),
        compiler_params=params(),
        name="pack",
    )(at, own, other)


def after(value, *others):
    return lax.optimization_barrier((value,) + others)[0]


def shards(
    tokens, routes, gate_fixed, up_weight, up_mask, down_weight, down_mask, threshold, cotangent
):
    owners = lax.axis_size("expert")
    ring = lax.axis_size("x")
    tok_rows, width = tokens.shape
    local_experts = up_weight.shape[0]
    experts = local_experts * owners
    capacity = (tok_rows * 5 + 2 * experts - 1) // (2 * experts)
    lanes = width // owners
    core = lax.axis_index("core")
    column = lax.axis_index("expert")
    here = lax.axis_index("x")
    inv_root = 1.0 / math.sqrt(width)
    right = [(i, (i + 1) % ring) for i in range(ring)]
    left = [(i, (i - 1) % ring) for i in range(ring)]
    across = [(i, (i + 2) % ring) for i in range(ring)]
    swap = [(0, 1), (1, 0)]

    cot_r = lax.ppermute(cotangent, "x", right)
    cot_l = lax.ppermute(cotangent, "x", left)
    mid = cotangent.shape[0] // 2
    cot_rr = lax.ppermute(cot_r[:mid], "x", right)
    cot_ll = lax.ppermute(cot_l[mid:], "x", left)

    by_tok = routes.T
    same = (by_tok[:, :, None, None] == by_tok[None, None]).astype(jnp.int32)
    before = jnp.arange(tok_rows)[:, None] < jnp.arange(tok_rows)[None, :]
    slot = jnp.sum(jnp.where(before[None, :, None, :], same, 0), axis=(0, 1))
    target = by_tok % local_experts * owners + by_tok // local_experts
    place = target * capacity + slot
    block = GROUP * capacity
    col = target * block + column % GROUP * capacity + slot

    meta = jnp.concatenate([col, gate_fixed.T, jnp.zeros((4, tok_rows), jnp.int32)], axis=0)
    meta = [meta] + [lax.ppermute(meta, "x", to) for to in (right, left, across)]
    meta = jnp.stack(meta, axis=0)

    take = jnp.arange(experts * capacity, dtype=jnp.int32)[:, None]
    pick = ((take == place[0][None]) | (take == place[1][None])).astype(BF)
    sent = jnp.dot(pick, tokens, preferred_element_type=F32).astype(BF)
    sent = sent.reshape(experts, capacity // 2, 2, width)
    arrived = lax.all_to_all(sent, PLANE, split_axis=0, concat_axis=0, tiled=True)
    ups = (up_weight, lax.ppermute(up_weight, "core", swap))
    downs = (down_weight, lax.ppermute(down_weight, "core", swap))
    small = jnp.concatenate(
        [up_mask.reshape(2, -1), down_mask.reshape(2, -1), threshold], axis=1
    )
    keep = lax.dynamic_index_in_dim(small, core, 0, keepdims=False)
    got = lax.ppermute(
        lax.dynamic_index_in_dim(small, 1 - core, 0, keepdims=False), "core", swap
    )
    n_up, n_down = up_mask[0].size, down_mask[0].size

    def piece(a):
        u = a[:n_up].reshape(up_mask.shape[1:])
        d = a[n_up : n_up + n_down].reshape(down_mask.shape[1:])
        return u, d, a[n_up + n_down :]

    pairs = [jnp.concatenate(p, axis=n) for p, n in zip(zip(piece(keep), piece(got)), (1, 0, 0))]
    masks = [jnp.repeat(p.astype(F32), SIDE, axis=1)[:, None, :] for p in pairs[:2]]
    scale = 4.0 / pairs[2].astype(F32)[None]
    core_at = core.reshape(1)

    x_own, masks, scale, cot_rr, cot_ll, meta = lax.optimization_barrier(
        (arrived.reshape(experts * capacity, width), masks, scale, cot_rr, cot_ll, meta)
    )
    x_r = lax.ppermute(x_own, "x", right)
    x_l = lax.ppermute(x_own, "x", left)

    meta = jnp.broadcast_to(after(meta, x_own)[None], (owners,) + meta.shape)
    meta = lax.all_to_all(meta, "expert", split_axis=0, concat_axis=0, tiled=True)

    cot_all = jnp.concatenate([cotangent, cot_r, cot_l, cot_rr, cot_ll], axis=0)
    built = grad_rows(meta, after(cot_all, x_own), experts, block)
    x_r, x_l, built = lax.optimization_barrier((x_r, x_l, built))
    grads = lax.all_to_all(built, PLANE, split_axis=0, concat_axis=0, tiled=True)

    mid = x_own.shape[0] // 2
    x_rh, x_lh = x_r[:mid], x_l[mid:]
    x_rr = lax.ppermute(x_rh, "x", right)
    x_ll = lax.ppermute(x_lh, "x", left)
    run = functools.partial(
        forward_rows, core=core_at, ups=ups, downs=downs, masks=masks, scale=scale, tiles=owners
    )
    so0, st0, p0a, p0b = run([after(x_own, x_rh, x_lh)], parts=2)
    so1, st1, lefta, leftb, righta, rightb = run([after(x_r, so0), x_l], parts=4)
    so2, st2, fara, farb = run([after(x_rr, so1), x_ll], parts=2)
    r_b = lax.ppermute(rightb, "x", right)
    l_a = lax.ppermute(lefta, "x", left)
    fara, farb = lax.optimization_barrier((fara, farb, r_b, l_a))[:2]
    r_far = lax.ppermute(fara, "x", right)
    l_far = lax.ppermute(farb, "x", left)

    def add(*v):
        return sum(a.astype(F32) for a in v).astype(BF)

    r_go, l_go = lax.optimization_barrier((add(righta, r_far), add(leftb, l_far)))
    r_a = lax.ppermute(r_go, "x", right)
    l_b = lax.ppermute(l_go, "x", left)

    summed = jnp.concatenate([add(p0a, r_a, l_a), add(p0b, r_b, l_b)], axis=0)
    back = lax.all_to_all(summed, PLANE, split_axis=0, concat_axis=0, tiled=True)

    slopes = (so0, st0, so1, st1, so2, st2)
    own, other = backward_rows(
        after(grads, r_go, l_go), core_at, downs, masks[1], slopes, (1, 2, 1)
    )
    other = lax.ppermute(other, "core", swap)

    mixed, gg = combine(meta, cotangent, after(back, own))
    gg_all = lax.all_to_all(gg, "expert", split_axis=0, concat_axis=0, tiled=True)
    from_shard = jnp.array([0, 2, 3, 1], jnp.int32)[(jnp.arange(ring) - here) % ring]
    at = jnp.concatenate([core.reshape(1), from_shard]).astype(jnp.int32)
    potential_grad = pack(at, after(own, gg), other, x_own.shape[0] // 2)
    gg_all = after(gg_all, potential_grad)
    gate_grad = (jnp.sum(gg_all, axis=0)[:2] * inv_root).T
    return (mixed, gate_grad, potential_grad)


def solution(mesh):
    devices = mesh.devices
    split = Mesh(
        devices.reshape(devices.shape[0] // 2, 2, devices.shape[1]), ("x", "core", "expert")
    )
    dp = ("x", "core")
    every = ("x", "core", "expert")
    placed = (
        P(every, None),
        P(every, None),
        P(every, None),
        P("expert", None, dp),
        P("expert", None, dp),
        P("expert", dp, None),
        P("expert", dp, None),
        P("expert", dp),
        P(dp, "expert"),
    )
    return jax.shard_map(
        shards,
        mesh=split,
        in_specs=placed,
        out_specs=(P(dp, "expert"), P(every, None), P(None, "expert", dp)),
        check_vma=False,
    )
```
